32 devices in a mesh: grp: 4 (over y, x), mem: 8 (over z, core).
Axes of the slice: x: 2, y: 2, z: 4, core: 2. Of those that a mesh axis runs over, the one named last changes fastest.
Arguments:
- points: float32 [512, 128], P(('grp', 'mem')), may hold values from -40 to 40, as said below
- slab: float32 [16384, 128], P('mem'), may hold values from -40 to 40, as said below
Outputs:
- new_points: float32 [512, 128], P(('grp', 'mem'))
The draws below stay inside these ranges and needn't reach their ends.
Inputs may be any that keep to these rules, and one draw needn't show every extreme that they name: Support points lie near the chains' centres. `slab`: each block of 2048 rows is one chain with its own centre and scale.
All inputs are finite; a program needn't handle non-finite values.
Results may differ from the reference program's by a relative error of at most 0.0001.
Values sent between devices are 32-bit elements; how exact they have to be, the bound alone decides.
A program may use at most 64 MiB of HBM per device.

```python
import jax
import jax.numpy as jnp
from jax import lax

D = 128
PT_DEV = 16
SAMP_DEV = 2048
NPTS = 512
NSAMP = 16384
N_GRP = 4
N_MEM = 8


def chain_centres(key):
    return 1.5 * jax.random.normal(jax.random.fold_in(key, 7), (N_MEM, D), jnp.float32)


def draw_slab(key, part):
    centres = chain_centres(key)
    scales = jnp.exp(jax.random.uniform(jax.random.fold_in(key, 11), (N_MEM,), jnp.float32, -0.7, 0.7))
    noise = jax.random.normal(jax.random.fold_in(key, 13), (N_MEM, SAMP_DEV, D), jnp.float32)
    values = centres[:, None, :] + scales[:, None, None] * noise
    return jnp.clip(values, -40.0, 40.0).reshape(N_MEM * SAMP_DEV, D)


def draw_points(key, part):
    centres = chain_centres(key)
    count = PT_DEV * N_GRP * N_MEM
    which = jax.random.randint(jax.random.fold_in(key, 19), (count,), 0, N_MEM)
    onehot = (which[:, None] == jnp.arange(N_MEM)[None, :]).astype(jnp.float32)
    noise = jax.random.normal(jax.random.fold_in(key, 23), (count, D), jnp.float32)
    values = jnp.dot(onehot, centres) + noise
    return jnp.clip(values, -40.0, 40.0)


def setup_inputs(seed: int = 0) -> dict:
    splits = jax.random.split(jax.random.key(seed), 3)
    return {
        "points": draw_points(jax.random.fold_in(splits[2], 71), 0),
        "slab": draw_slab(jax.random.fold_in(splits[2], 71), 0),
    }


def weights_of(left, right_operand):
    left_square_norm = lax.optimization_barrier(jnp.sum(jnp.square(left), axis=1))
    right_square_norm = lax.optimization_barrier(jnp.sum(jnp.square(right_operand), axis=1))
    cross_product = jnp.dot(left, right_operand.T, precision=lax.Precision.HIGHEST, preferred_element_type=jnp.float32)
    squared_distance = left_square_norm[:, None] + right_square_norm[None, :] - 2.0 * cross_product
    return 1.0 / jnp.sqrt(squared_distance + 1.0)

def reference(points, slab):
    ratio = NSAMP / NPTS
    support_point_block = min(NPTS, 512)
    sblock = min(NSAMP, 512)
    slab_blocks = slab.reshape(NSAMP // sblock, sblock, D)

    def one_block(block):

        def step(carry, rows):
            numer, total = carry
            wts = weights_of(block, rows)
            numer = numer + jnp.dot(wts, rows, precision=lax.Precision.HIGHEST, preferred_element_type=jnp.float32)
            total = total + lax.optimization_barrier(jnp.sum(wts, axis=1))
            return ((numer, total), None)
        init = (jnp.zeros((support_point_block, D), jnp.float32), jnp.zeros((support_point_block,), jnp.float32))
        (numer, total), _ = lax.scan(step, init, slab_blocks)
        pw = weights_of(block, points)
        pair_vec = jnp.dot(pw, points, precision=lax.Precision.HIGHEST, preferred_element_type=jnp.float32)
        pair_sum = lax.optimization_barrier(jnp.sum(pw, axis=1))
        repel = block * pair_sum[:, None] - pair_vec
        return (ratio * repel + numer) / total[:, None]
    update_output = lax.map(one_block, points.reshape(NPTS // support_point_block, support_point_block, D))
    return update_output.reshape(NPTS, D)
```

```python
import functools

import jax
import jax.numpy as jnp
from jax import lax
from jax.experimental import pallas as pl
from jax.experimental.pallas import tpu as pltpu
from jax.sharding import PartitionSpec as P

MESH = pl.DeviceIdType.MESH
NT = (((1,), (1,)), ((), ()))
LANES = 128


def split3(x):
    hi = x.astype(jnp.bfloat16)
    rest = x - hi.astype(jnp.float32)
    mid = rest.astype(jnp.bfloat16)
    low = (rest - mid.astype(jnp.float32)).astype(jnp.bfloat16)
    return hi, mid, low


def split2(x):
    hi = x.astype(jnp.bfloat16)
    return hi, (x - hi.astype(jnp.float32)).astype(jnp.bfloat16)


def ndot(left, right):
    return lax.dot_general(left, right, NT, preferred_element_type=jnp.float32)


def prep_rows(rows):
    hi, mid, low = split3(rows)
    q1, q2, q3 = split3(rows * rows)
    ones = jnp.ones((8, rows.shape[1]), jnp.bfloat16)
    norm = ndot(ones, q1) + (ndot(ones, q2) + ndot(ones, q3))
    return (
        jnp.concatenate([hi, mid], axis=1),
        jnp.concatenate([low, hi], axis=1),
        norm,
    )


def kernel(
    ng, nm, ratio, chunk,
    pts_hbm, slab_hbm, out_ref,
    gp, cp, slab_v, b12, b31, bn, sendbuf, recvbuf,
    loc_sem, slab_sem, gsend, grecv, csend, crecv, rsend, rrecv,
):
    g = lax.axis_index("grp")
    m = lax.axis_index("mem")
    owned, width = pts_hbm.shape
    rows = slab_hbm.shape[0]
    n_chunk = rows // chunk
    mem_peer = [lax.rem(m + j, nm) for j in range(nm)]
    grp_peer = [lax.rem(g + j, ng) for j in range(ng)]

    barrier = pltpu.get_barrier_semaphore()
    for j in range(1, nm):
        pl.semaphore_signal(barrier, inc=1, device_id=(g, mem_peer[j]), device_id_type=MESH)
    for j in range(1, ng):
        pl.semaphore_signal(barrier, inc=1, device_id=(grp_peer[j], m), device_id_type=MESH)

    own_g = pltpu.make_async_copy(pts_hbm, gp.at[m], loc_sem.at[0])
    own_c = pltpu.make_async_copy(pts_hbm, cp.at[g], loc_sem.at[1])
    own_g.start()
    own_c.start()
    slab_copies = []
    for c in range(n_chunk):
        part = pl.ds(c * chunk, chunk)
        copy = pltpu.make_async_copy(slab_hbm.at[part], slab_v.at[part], slab_sem.at[c])
        copy.start()
        slab_copies.append(copy)
    pad = cp.shape[0] - ng
    if pad:
        cp[pl.ds(ng, pad)] = jnp.zeros((pad, owned, width), jnp.float32)

    own_g.wait()
    own_c.wait()
    pl.semaphore_wait(barrier, nm + ng - 2)

    sends = []
    for j in range(1, nm):
        copy = pltpu.make_async_remote_copy(
            src_ref=gp.at[m], dst_ref=gp.at[m],
            send_sem=gsend.at[j], recv_sem=grecv.at[j],
            device_id=(g, mem_peer[j]), device_id_type=MESH,
        )
        copy.start()
        sends.append(copy)
    for j in range(1, ng):
        copy = pltpu.make_async_remote_copy(
            src_ref=cp.at[g], dst_ref=cp.at[g],
            send_sem=csend.at[j], recv_sem=crecv.at[j],
            device_id=(grp_peer[j], m), device_id_type=MESH,
        )
        copy.start()
        sends.append(copy)

    for c in range(n_chunk):
        part = pl.ds(c * chunk, chunk)
        slab_copies[c].wait()
        b12[part], b31[part], bn[:, part] = prep_rows(slab_v[part])

    for copy in sends:
        copy.wait_recv()

    pts = gp[...].reshape(nm * owned, width)
    count = nm * owned
    norm1 = jnp.sum(pts * pts, axis=1, keepdims=True) + 1.0
    p1, p2, p3 = split3(-2.0 * pts)
    left12 = jnp.concatenate(
        [jnp.concatenate([p1, p1], axis=1), jnp.concatenate([p2, p2], axis=1)], axis=0
    )
    left31 = jnp.concatenate([p1, p3], axis=1)

    def weights(r12, r31, norms):
        both = ndot(left12, r12)
        cross = both[:count] + both[count:] + ndot(left31, r31)
        return lax.rsqrt(norm1 + norms + cross)

    def folded(w):
        total = w[:, :LANES]
        for k in range(1, w.shape[1] // LANES):
            total = total + w[:, k * LANES:(k + 1) * LANES]
        return total

    def accum(w, r12):
        return jnp.dot(
            jnp.concatenate(split2(w), axis=0), r12, preferred_element_type=jnp.float32
        )

    pair_rows = cp[...].reshape(cp.shape[0] * owned, width)
    r12, r31, norms = prep_rows(pair_rows)
    w = weights(r12, r31, norms[0:1])
    if pad:
        lane = lax.broadcasted_iota(jnp.int32, w.shape, 1)
        w = jnp.where(lane < ng * owned, w, 0.0)
    pair_part = folded(w)
    acc = accum(w * (-ratio), r12)
    weight_part = None
    for c in range(n_chunk):
        part = pl.ds(c * chunk, chunk)
        r12 = b12[part]
        w = weights(r12, b31[part], bn[0:1, part])
        weight_part = folded(w) if weight_part is None else weight_part + folded(w)
        acc = acc + accum(w, r12)
    acc = acc[:count] + acc[count:]
    acc = acc[:, :width] + acc[:, width:]
    weight_row = jnp.sum(weight_part.T, axis=0, keepdims=True)
    pair_row = jnp.sum(pair_part.T, axis=0, keepdims=True)
    for t in range(nm):
        seg = pl.ds((t * owned) // LANES * LANES, LANES)
        lo = (t * owned) // LANES * LANES
        sendbuf[t, 0:owned] = acc[t * owned:(t + 1) * owned]
        sendbuf[t, owned:owned + 1] = weight_row[:, lo:lo + LANES]
        sendbuf[t, owned + 1:owned + 2] = pair_row[:, lo:lo + LANES]

    outs = []
    for j in range(1, nm):
        copy = pltpu.make_async_remote_copy(
            src_ref=sendbuf.at[mem_peer[j], pl.ds(0, owned + 2)],
            dst_ref=recvbuf.at[j, pl.ds(0, owned + 2)],
            send_sem=rsend.at[j], recv_sem=rrecv.at[j],
            device_id=(g, mem_peer[j]), device_id_type=MESH,
        )
        copy.start()
        outs.append(copy)
    for copy in outs:
        copy.wait_recv()
    vec = sendbuf[m, 0:owned]
    sums = sendbuf[m, owned:owned + 2]
    for j in range(1, nm):
        vec = vec + recvbuf[j, 0:owned]
        sums = sums + recvbuf[j, owned:owned + 2]
    lane = lax.broadcasted_iota(jnp.int32, (owned, LANES), 1)
    row = lax.broadcasted_iota(jnp.int32, (owned, LANES), 0)
    mine = lane == row + lax.rem(m * owned, LANES)
    weight = jnp.sum(jnp.where(mine, sums[0:1], 0.0), axis=1, keepdims=True)
    pair = jnp.sum(jnp.where(mine, sums[1:2], 0.0), axis=1, keepdims=True)
    out_ref[...] = (gp[m] * (ratio * pair) + vec) / weight
    for copy in sends + outs:
        copy.wait_send()


def shards(points, slab):
    owned, width = points.shape
    rows = slab.shape[0]
    ng, nm = lax.axis_size("grp"), lax.axis_size("mem")
    ratio = rows / (owned * ng)
    chunk = min(rows, 512)
    n_chunk = rows // chunk
    pair_slots = -(-ng * owned // LANES) * LANES // owned
    sem = pltpu.SemaphoreType.DMA
    return pl.pallas_call(
        functools.partial(kernel, ng, nm, ratio, chunk),
        out_shape=jax.ShapeDtypeStruct((owned, width), jnp.float32),
        in_specs=[pl.BlockSpec(memory_space=pl.ANY)] * 2,
        out_specs=pl.BlockSpec(memory_space=pltpu.VMEM),
        scratch_shapes=[
            pltpu.VMEM((nm, owned, width), jnp.float32),
            pltpu.VMEM((pair_slots, owned, width), jnp.float32),
            pltpu.VMEM((rows, width), jnp.float32),
            pltpu.VMEM((rows, 2 * width), jnp.bfloat16),
            pltpu.VMEM((rows, 2 * width), jnp.bfloat16),
            pltpu.VMEM((8, rows), jnp.float32),
            pltpu.VMEM((nm, owned + 8, width), jnp.float32),
            pltpu.VMEM((nm, owned + 8, width), jnp.float32),
            sem((2,)), sem((n_chunk,)),
            sem((nm,)), sem((nm,)), sem((ng,)), sem((ng,)), sem((nm,)), sem((nm,)),
        ],
        compiler_params=pltpu.CompilerParams(collective_id=0, has_side_effects=True),
    )(points, slab)


def solution(mesh):
    placed = (P(("grp", "mem"), None), P("mem", None))
    return jax.shard_map(
        shards, mesh=mesh, in_specs=placed, out_specs=P(("grp", "mem"), None), check_vma=False
    )
```

```python
import functools

import jax
import jax.numpy as jnp
from jax import lax
from jax.experimental import pallas as pl
from jax.experimental.pallas import tpu as pltpu
from jax.sharding import PartitionSpec as P

MESH = pl.DeviceIdType.MESH
NT = (((1,), (1,)), ((), ()))
LANES = 128
LEAD = 4


def split3(x):
    hi = x.astype(jnp.bfloat16)
    rest = x - hi.astype(jnp.float32)
    mid = rest.astype(jnp.bfloat16)
    low = (rest - mid.astype(jnp.float32)).astype(jnp.bfloat16)
    return hi, mid, low


def split2(x):
    hi = x.astype(jnp.bfloat16)
    return hi, (x - hi.astype(jnp.float32)).astype(jnp.bfloat16)


def ndot(left, right):
    return lax.dot_general(left, right, NT, preferred_element_type=jnp.float32)


def prep_rows(rows):
    hi, mid, low = split3(rows)
    q1, q2, q3 = split3(rows * rows)
    ones = jnp.ones((8, rows.shape[1]), jnp.bfloat16)
    norm = ndot(ones, q1) + (ndot(ones, q2) + ndot(ones, q3))
    return (
        jnp.concatenate([hi, mid], axis=1),
        jnp.concatenate([low, hi], axis=1),
        norm,
    )


def kernel(
    ng, nm, ratio, chunk,
    pts_hbm, slab_hbm, out_ref,
    gp, cp, slab_v, b12, b31, bn, sendbuf, recvbuf,
    loc_sem, slab_sem, ready, cready, gsend, grecv, psend, csend, crecv, rsend, rrecv,
):
    g = lax.axis_index("grp")
    m = lax.axis_index("mem")
    owned, width = pts_hbm.shape
    rows = slab_hbm.shape[0]
    n_chunk = rows // chunk
    mem_up = [jnp.minimum(m + j, nm - 1) for j in range(nm)]
    mem_down = [jnp.maximum(m - j, 0) for j in range(nm)]
    grp_up = [jnp.minimum(g + j, ng - 1) for j in range(ng)]
    grp_down = [jnp.maximum(g - j, 0) for j in range(ng)]
    odd = lax.rem(m, 2) == 1
    even = jnp.logical_not(odd)

    def both(*conds):
        return functools.reduce(jnp.logical_and, conds)

    def greet(semaphore, device):
        pl.semaphore_signal(semaphore, inc=1, device_id=device, device_id_type=MESH)

    barrier = pltpu.get_barrier_semaphore()
    for j in range(1, nm):
        pl.when(m + j < nm)(lambda j=j: greet(barrier, (g, mem_up[j])))
    for j in range(1, ng):
        pl.when(g + j < ng)(lambda j=j: greet(barrier, (grp_up[j], m)))

    own_g = pltpu.make_async_copy(pts_hbm, gp.at[m], loc_sem.at[0])
    own_c = pltpu.make_async_copy(pts_hbm, cp.at[g], loc_sem.at[1])
    own_g.start()
    own_c.start()
    slab_copy = pltpu.make_async_copy(slab_hbm, slab_v, slab_sem)
    slab_copy.start()
    pad = cp.shape[0] - ng
    if pad:
        cp[pl.ds(ng, pad)] = jnp.zeros((pad, owned, width), jnp.float32)

    pl.when(m + g > 0)(lambda: pl.semaphore_wait(barrier, m + g))
    for j in reversed(range(1, nm)):
        pl.when(m >= j)(lambda j=j: greet(ready.at[j - 1], (g, mem_down[j])))
    for j in reversed(range(1, ng)):
        pl.when(g >= j)(lambda j=j: greet(cready.at[j - 1], (grp_down[j], m)))

    def remote(src, dst, send_sem, recv_sem, device):
        return pltpu.make_async_remote_copy(
            src_ref=src, dst_ref=dst, send_sem=send_sem, recv_sem=recv_sem,
            device_id=device, device_id_type=MESH,
        )

    def own_up(j):
        return remote(pts_hbm, gp.at[m], gsend.at[j - 1], grecv.at[j - 1], (g, mem_up[j]))

    def own_down(j):
        d = nm - j
        return remote(pts_hbm, gp.at[m], gsend.at[d - 1], grecv.at[d - 1], (g, mem_down[j]))

    def pass_up(back, j, slot):
        block = gp.at[mem_down[back]]
        return remote(block, block, psend.at[slot], grecv.at[back + j - 1], (g, mem_up[j]))

    def pair_up(j):
        return remote(pts_hbm, cp.at[g], csend, crecv, (grp_up[j], m))

    def pair_down(j):
        return remote(pts_hbm, cp.at[g], csend, crecv, (grp_down[j], m))

    def take(owner, d):
        block = gp.at[owner]
        pltpu.make_async_copy(block, block, grecv.at[d - 1]).wait()

    sent = []

    def send(cond, make, *args):
        pl.when(cond)(lambda: make(*args).start())
        sent.append((cond, make, args))

    for j in reversed(range(1, nm)):
        send(m >= j, own_down, j)
    for j in range(1, ng):
        pl.when(g >= j)(lambda j=j: pair_down(j).start())

    early_mate = both(odd, m + 2 < nm)
    early_pass = both(odd, m >= 3, m + 3 < nm)
    slot = 1
    for j in range(1, nm):
        pl.when(m + j < nm)(lambda j=j: pl.semaphore_wait(ready.at[j - 1], 1))
        if j in (1, 2, 4):
            send(m + j < nm, own_up, j)
        elif j == 3:
            send(both(odd, m + j < nm), own_up, j)
        elif j == 5:
            send(both(even, m + j < nm), own_up, j)
        if j == 2:
            pl.when(early_mate)(lambda: take(mem_down[1], 1))
            send(early_mate, pass_up, 1, 2, 0)
        if j == 3:
            @pl.when(early_pass)
            def _():
                take(mem_down[2], 2)
                take(mem_down[3], 3)
        if 3 <= j < nm - 3:
            for back in (3, 2):
                send(both(early_pass, m + j < nm), pass_up, back, j, slot)
                slot += 1
    for k in range(1, ng):
        pl.when(g + k < ng)(lambda k=k: pl.semaphore_wait(cready.at[k - 1], 1))
        pl.when(g + k < ng)(lambda k=k: pair_up(k).start())

    slab_copy.wait()
    for c in range(n_chunk):
        part = pl.ds(c * chunk, chunk)
        b12[part], b31[part], bn[:, part] = prep_rows(slab_v[part])
    own_g.wait()
    own_c.wait()
    pair_blocks = cp.at[pl.ds(0, ng - 1)]
    pltpu.make_async_copy(pair_blocks, pair_blocks, crecv).wait()
    pair_rows = cp[...].reshape(cp.shape[0] * owned, width)
    pair12, pair31, pair_norms = prep_rows(pair_rows)

    def row_of(part):
        short = -part.shape[0] % LANES
        if short:
            part = jnp.concatenate([part, jnp.zeros((short, LANES), jnp.float32)], axis=0)
        return jnp.sum(part.T, axis=0, keepdims=True)

    def folded(w):
        total = w[:, :LANES]
        for k in range(1, w.shape[1] // LANES):
            total = total + w[:, k * LANES:(k + 1) * LANES]
        return total

    def accum(w, r12):
        return jnp.dot(
            jnp.concatenate(split2(w), axis=0), r12, preferred_element_type=jnp.float32
        )

    def partial_sums(first, blocks):
        for owner in range(first, first + blocks):
            d = lax.rem(m - owner + nm, nm)
            waited = jnp.logical_or(
                both(early_mate, d == 1), both(early_pass, jnp.logical_or(d == 2, d == 3))
            )
            pl.when(both(d > 0, jnp.logical_not(waited)))(
                lambda owner=owner, d=d: take(owner, jnp.maximum(d, 1))
            )
        count = blocks * owned
        pts = gp[first:first + blocks].reshape(count, width)
        norm1 = jnp.sum(pts * pts, axis=1, keepdims=True) + 1.0
        p1, p2, p3 = split3(-2.0 * pts)
        left12 = jnp.concatenate(
            [jnp.concatenate([p1, p1], axis=1), jnp.concatenate([p2, p2], axis=1)], axis=0
        )
        left31 = jnp.concatenate([p1, p3], axis=1)

        def weights(r12, r31, norms):
            twice = ndot(left12, r12)
            cross = twice[:count] + twice[count:] + ndot(left31, r31)
            return lax.rsqrt(norm1 + norms + cross)

        w = weights(pair12, pair31, pair_norms[0:1])
        if pad:
            lane = lax.broadcasted_iota(jnp.int32, w.shape, 1)
            w = jnp.where(lane < ng * owned, w, 0.0)
        pair_part = folded(w)
        acc = accum(w * (-ratio), pair12)
        weight_part = None
        for c in range(n_chunk):
            part = pl.ds(c * chunk, chunk)
            r12 = b12[part]
            w = weights(r12, b31[part], bn[0:1, part])
            weight_part = folded(w) if weight_part is None else weight_part + folded(w)
            acc = acc + accum(w, r12)
        acc = acc[:count] + acc[count:]
        acc = acc[:, :width] + acc[:, width:]
        weight_row = row_of(weight_part)
        pair_row = row_of(pair_part)
        for b in range(blocks):
            t = first + b
            lo = (b * owned) // LANES * LANES
            sendbuf[t, 0:owned] = acc[b * owned:(b + 1) * owned]
            sendbuf[t, owned:owned + 1] = weight_row[:, lo:lo + LANES]
            sendbuf[t, owned + 1:owned + 2] = pair_row[:, lo:lo + LANES]
        for t in range(first, first + blocks):
            slot = lax.rem(t - m + nm, nm)
            pl.when(slot > 0)(lambda t=t, slot=slot: remote(
                sendbuf.at[t, pl.ds(0, owned + 2)], recvbuf.at[slot, pl.ds(0, owned + 2)],
                rsend, rrecv, (g, t),
            ).start())

    lead = min(LEAD, nm)
    if lead:
        partial_sums(0, lead)
    partial_sums(lead, nm - lead)

    filled = recvbuf.at[pl.ds(1, nm - 1), pl.ds(0, owned + 2)]
    pltpu.make_async_copy(filled, filled, rrecv).wait()
    vec = sendbuf[m, 0:owned]
    sums = sendbuf[m, owned:owned + 2]
    for j in range(1, nm):
        vec = vec + recvbuf[j, 0:owned]
        sums = sums + recvbuf[j, owned:owned + 2]
    lane = lax.broadcasted_iota(jnp.int32, (owned, LANES), 1)
    row = lax.broadcasted_iota(jnp.int32, (owned, LANES), 0)
    place = jnp.where(m < lead, m, m - lead)
    mine = lane == row + lax.rem(place * owned, LANES)
    weight = jnp.sum(jnp.where(mine, sums[0:1], 0.0), axis=1, keepdims=True)
    pair = jnp.sum(jnp.where(mine, sums[1:2], 0.0), axis=1, keepdims=True)
    out_ref[...] = (gp[m] * (ratio * pair) + vec) / weight
    pltpu.make_async_copy(filled, filled, rsend).wait()
    pltpu.make_async_copy(pair_blocks, pair_blocks, csend).wait()
    for cond, make, args in sent:
        pl.when(cond)(lambda make=make, args=args: make(*args).wait_send())


def shards(points, slab):
    owned, width = points.shape
    rows = slab.shape[0]
    ng, nm = lax.axis_size("grp"), lax.axis_size("mem")
    ratio = rows / (owned * ng)
    chunk = min(rows, 512)
    pair_slots = -(-ng * owned // LANES) * LANES // owned
    sem = pltpu.SemaphoreType.DMA
    return pl.pallas_call(
        functools.partial(kernel, ng, nm, ratio, chunk),
        out_shape=pltpu.VMEM((owned, width), jnp.float32),
        in_specs=[pl.BlockSpec(memory_space=pl.ANY)] * 2,
        out_specs=pl.BlockSpec(memory_space=pltpu.VMEM),
        scratch_shapes=[
            pltpu.VMEM((nm, owned, width), jnp.float32),
            pltpu.VMEM((pair_slots, owned, width), jnp.float32),
            pltpu.VMEM((rows, width), jnp.float32),
            pltpu.VMEM((rows, 2 * width), jnp.bfloat16),
            pltpu.VMEM((rows, 2 * width), jnp.bfloat16),
            pltpu.VMEM((8, rows), jnp.float32),
            pltpu.VMEM((nm, owned + 8, width), jnp.float32),
            pltpu.VMEM((nm, owned + 8, width), jnp.float32),
            sem((2,)), sem,
            pltpu.SemaphoreType.REGULAR((nm - 1,)), pltpu.SemaphoreType.REGULAR((ng - 1,)),
            sem((nm - 1,)), sem((nm - 1,)), sem((max(1, 1 + 2 * (nm - 6)),)),
            sem, sem, sem, sem,
        ],
        compiler_params=pltpu.CompilerParams(collective_id=0, has_side_effects=True),
    )(points, slab)


def solution(mesh):
    placed = (P(("grp", "mem"), None), P("mem", None))
    return jax.shard_map(
        shards, mesh=mesh, in_specs=placed, out_specs=P(("grp", "mem"), None), check_vma=False
    )
```

```python
import functools

import jax
import jax.numpy as jnp
from jax import lax
from jax.experimental import pallas as pl
from jax.experimental.pallas import tpu as pltpu
from jax.sharding import PartitionSpec as P

MESH = pl.DeviceIdType.MESH
NT = (((1,), (1,)), ((), ()))
LANES = 128
LEAD = 4


def split3(x):
    hi = x.astype(jnp.bfloat16)
    rest = x - hi.astype(jnp.float32)
    mid = rest.astype(jnp.bfloat16)
    low = (rest - mid.astype(jnp.float32)).astype(jnp.bfloat16)
    return hi, mid, low


def split2(x):
    hi = x.astype(jnp.bfloat16)
    return hi, (x - hi.astype(jnp.float32)).astype(jnp.bfloat16)


def ndot(left, right):
    return lax.dot_general(left, right, NT, preferred_element_type=jnp.float32)


def prep_rows(rows):
    hi, mid, low = split3(rows)
    q1, q2, q3 = split3(rows * rows)
    ones = jnp.ones((8, rows.shape[1]), jnp.bfloat16)
    norm = ndot(ones, q1) + (ndot(ones, q2) + ndot(ones, q3))
    return (
        jnp.concatenate([hi, mid], axis=1),
        jnp.concatenate([low, hi], axis=1),
        norm,
    )


def kernel(
    ng, nm, ratio, chunk,
    pts_hbm, slab_hbm, out_ref,
    gp, cp, slab_v, b12, b31, bn, sendbuf, recvbuf,
    loc_sem, slab_sem, ready, cready, gsend, grecv, psend, csend, crecv, rsend, rrecv,
):
    g = lax.axis_index("grp")
    m = lax.axis_index("mem")
    owned, width = pts_hbm.shape
    rows = slab_hbm.shape[0]
    n_chunk = rows // chunk
    mem_up = [jnp.minimum(m + j, nm - 1) for j in range(nm)]
    mem_down = [jnp.maximum(m - j, 0) for j in range(nm)]
    grp_up = [jnp.minimum(g + j, ng - 1) for j in range(ng)]
    grp_down = [jnp.maximum(g - j, 0) for j in range(ng)]
    odd = lax.rem(m, 2) == 1
    even = jnp.logical_not(odd)

    def both(*conds):
        return functools.reduce(jnp.logical_and, conds)

    def greet(semaphore, device):
        pl.semaphore_signal(semaphore, inc=1, device_id=device, device_id_type=MESH)

    barrier = pltpu.get_barrier_semaphore()
    for j in range(1, nm):
        pl.when(m + j < nm)(lambda j=j: greet(barrier, (g, mem_up[j])))
    for j in range(1, ng):
        pl.when(g + j < ng)(lambda j=j: greet(barrier, (grp_up[j], m)))

    own_g = pltpu.make_async_copy(pts_hbm, gp.at[m], loc_sem.at[0])
    own_c = pltpu.make_async_copy(pts_hbm, cp.at[g], loc_sem.at[1])
    own_g.start()
    own_c.start()
    slab_copy = pltpu.make_async_copy(slab_hbm, slab_v, slab_sem)
    slab_copy.start()
    pad = cp.shape[0] - ng
    if pad:
        cp[pl.ds(ng, pad)] = jnp.zeros((pad, owned, width), jnp.float32)

    pl.when(m + g > 0)(lambda: pl.semaphore_wait(barrier, m + g))
    for j in reversed(range(1, nm)):
        pl.when(m >= j)(lambda j=j: greet(ready.at[j - 1], (g, mem_down[j])))
    for j in reversed(range(1, ng)):
        pl.when(g >= j)(lambda j=j: greet(cready.at[j - 1], (grp_down[j], m)))

    def remote(src, dst, send_sem, recv_sem, device):
        return pltpu.make_async_remote_copy(
            src_ref=src, dst_ref=dst, send_sem=send_sem, recv_sem=recv_sem,
            device_id=device, device_id_type=MESH,
        )

    def own_up(j):
        return remote(pts_hbm, gp.at[m], gsend.at[j - 1], grecv.at[j - 1], (g, mem_up[j]))

    def own_down(j):
        d = nm - j
        return remote(pts_hbm, gp.at[m], gsend.at[d - 1], grecv.at[d - 1], (g, mem_down[j]))

    def pass_up(back, j, slot):
        block = gp.at[mem_down[back]]
        return remote(block, block, psend.at[slot], grecv.at[back + j - 1], (g, mem_up[j]))

    def pair_up(j):
        return remote(pts_hbm, cp.at[g], csend, crecv, (grp_up[j], m))

    def pair_down(j):
        return remote(pts_hbm, cp.at[g], csend, crecv, (grp_down[j], m))

    def take(owner, d):
        block = gp.at[owner]
        pltpu.make_async_copy(block, block, grecv.at[d - 1]).wait()

    sent = []

    def send(cond, make, *args):
        pl.when(cond)(lambda: make(*args).start())
        sent.append((cond, make, args))

    for j in reversed(range(1, nm)):
        send(m >= j, own_down, j)
    for j in range(1, ng):
        pl.when(g >= j)(lambda j=j: pair_down(j).start())

    early_mate = both(odd, m + 2 < nm)
    early_pass = both(odd, m >= 3, m + 3 < nm)
    slot = 1
    for j in range(1, nm):
        pl.when(m + j < nm)(lambda j=j: pl.semaphore_wait(ready.at[j - 1], 1))
        if j in (1, 2, 4):
            send(m + j < nm, own_up, j)
        elif j == 3:
            send(both(odd, m + j < nm), own_up, j)
        elif j == 5:
            send(both(even, m + j < nm), own_up, j)
        if j == 2:
            pl.when(early_mate)(lambda: take(mem_down[1], 1))
            send(early_mate, pass_up, 1, 2, 0)
        if j == 3:
            @pl.when(early_pass)
            def _():
                take(mem_down[2], 2)
                take(mem_down[3], 3)
        if 3 <= j < nm - 3:
            for back in (3, 2):
                send(both(early_pass, m + j < nm), pass_up, back, j, slot)
                slot += 1
    for k in range(1, ng):
        pl.when(g + k < ng)(lambda k=k: pl.semaphore_wait(cready.at[k - 1], 1))
        pl.when(g + k < ng)(lambda k=k: pair_up(k).start())

    slab_copy.wait()
    for c in range(n_chunk):
        part = pl.ds(c * chunk, chunk)
        b12[part], b31[part], bn[:, part] = prep_rows(slab_v[part])
    own_g.wait()
    own_c.wait()
    pair_blocks = cp.at[pl.ds(0, ng - 1)]
    pltpu.make_async_copy(pair_blocks, pair_blocks, crecv).wait()
    pair_rows = cp[...].reshape(cp.shape[0] * owned, width)
    pair12, pair31, pair_norms = prep_rows(pair_rows)

    def row_of(part):
        short = -part.shape[0] % LANES
        if short:
            part = jnp.concatenate([part, jnp.zeros((short, LANES), jnp.float32)], axis=0)
        return jnp.sum(part.T, axis=0, keepdims=True)

    def folded(w):
        total = w[:, :LANES]
        for k in range(1, w.shape[1] // LANES):
            total = total + w[:, k * LANES:(k + 1) * LANES]
        return total

    def accum(w, r12):
        return jnp.dot(
            jnp.concatenate(split2(w), axis=0), r12, preferred_element_type=jnp.float32
        )

    def partial_sums(first, blocks):
        for owner in range(first, first + blocks):
            d = lax.rem(m - owner + nm, nm)
            waited = jnp.logical_or(
                both(early_mate, d == 1), both(early_pass, jnp.logical_or(d == 2, d == 3))
            )
            pl.when(both(d > 0, jnp.logical_not(waited)))(
                lambda owner=owner, d=d: take(owner, jnp.maximum(d, 1))
            )
        count = blocks * owned
        pts = gp[first:first + blocks].reshape(count, width)
        norm1 = jnp.sum(pts * pts, axis=1, keepdims=True) + 1.0
        p1, p2, p3 = split3(-2.0 * pts)
        left12 = jnp.concatenate(
            [jnp.concatenate([p1, p1], axis=1), jnp.concatenate([p2, p2], axis=1)], axis=0
        )
        left31 = jnp.concatenate([p1, p3], axis=1)

        def weights(r12, r31, norms):
            twice = ndot(left12, r12)
            cross = twice[:count] + twice[count:] + ndot(left31, r31)
            return lax.rsqrt(norm1 + norms + cross)

        w = weights(pair12, pair31, pair_norms[0:1])
        if pad:
            lane = lax.broadcasted_iota(jnp.int32, w.shape, 1)
            w = jnp.where(lane < ng * owned, w, 0.0)
        pair_part = folded(w)
        acc = accum(w * (-ratio), pair12)
        weight_part = None
        parts = [pl.ds(c * chunk, chunk) for c in range(n_chunk)]
        all_w = [weights(b12[part], b31[part], bn[0:1, part]) for part in parts]
        for w, part in zip(all_w, parts):
            weight_part = folded(w) if weight_part is None else weight_part + folded(w)
            acc = acc + accum(w, b12[part])
        acc = acc[:count] + acc[count:]
        acc = acc[:, :width] + acc[:, width:]
        weight_row = row_of(weight_part)
        pair_row = row_of(pair_part)
        for b in range(blocks):
            t = first + b
            lo = (b * owned) // LANES * LANES
            sendbuf[t, 0:owned] = acc[b * owned:(b + 1) * owned]
            sendbuf[t, owned:owned + 1] = weight_row[:, lo:lo + LANES]
            sendbuf[t, owned + 1:owned + 2] = pair_row[:, lo:lo + LANES]
        for t in range(first, first + blocks):
            slot = lax.rem(t - m + nm, nm)
            pl.when(slot > 0)(lambda t=t, slot=slot: remote(
                sendbuf.at[t, pl.ds(0, owned + 2)], recvbuf.at[slot, pl.ds(0, owned + 2)],
                rsend, rrecv, (g, t),
            ).start())

    lead = min(LEAD, nm)
    if lead:
        partial_sums(0, lead)
    partial_sums(lead, nm - lead)

    filled = recvbuf.at[pl.ds(1, nm - 1), pl.ds(0, owned + 2)]
    pltpu.make_async_copy(filled, filled, rrecv).wait()
    vec = sendbuf[m, 0:owned]
    sums = sendbuf[m, owned:owned + 2]
    for j in range(1, nm):
        vec = vec + recvbuf[j, 0:owned]
        sums = sums + recvbuf[j, owned:owned + 2]
    lane = lax.broadcasted_iota(jnp.int32, (owned, LANES), 1)
    row = lax.broadcasted_iota(jnp.int32, (owned, LANES), 0)
    place = jnp.where(m < lead, m, m - lead)
    mine = lane == row + lax.rem(place * owned, LANES)
    weight = jnp.sum(jnp.where(mine, sums[0:1], 0.0), axis=1, keepdims=True)
    pair = jnp.sum(jnp.where(mine, sums[1:2], 0.0), axis=1, keepdims=True)
    out_ref[...] = (gp[m] * (ratio * pair) + vec) / weight
    pltpu.make_async_copy(filled, filled, rsend).wait()
    pltpu.make_async_copy(pair_blocks, pair_blocks, csend).wait()
    for cond, make, args in sent:
        pl.when(cond)(lambda make=make, args=args: make(*args).wait_send())


def shards(points, slab):
    owned, width = points.shape
    rows = slab.shape[0]
    ng, nm = lax.axis_size("grp"), lax.axis_size("mem")
    ratio = rows / (owned * ng)
    chunk = min(rows, 256)
    pair_slots = -(-ng * owned // LANES) * LANES // owned
    sem = pltpu.SemaphoreType.DMA
    return pl.pallas_call(
        functools.partial(kernel, ng, nm, ratio, chunk),
        out_shape=pltpu.VMEM((owned, width), jnp.float32),
        in_specs=[pl.BlockSpec(memory_space=pl.ANY)] * 2,
        out_specs=pl.BlockSpec(memory_space=pltpu.VMEM),
        scratch_shapes=[
            pltpu.VMEM((nm, owned, width), jnp.float32),
            pltpu.VMEM((pair_slots, owned, width), jnp.float32),
            pltpu.VMEM((rows, width), jnp.float32),
            pltpu.VMEM((rows, 2 * width), jnp.bfloat16),
            pltpu.VMEM((rows, 2 * width), jnp.bfloat16),
            pltpu.VMEM((8, rows), jnp.float32),
            pltpu.VMEM((nm, owned + 8, width), jnp.float32),
            pltpu.VMEM((nm, owned + 8, width), jnp.float32),
            sem((2,)), sem,
            pltpu.SemaphoreType.REGULAR((nm - 1,)), pltpu.SemaphoreType.REGULAR((ng - 1,)),
            sem((nm - 1,)), sem((nm - 1,)), sem((max(1, 1 + 2 * (nm - 6)),)),
            sem, sem, sem, sem,
        ],
        compiler_params=pltpu.CompilerParams(collective_id=0, has_side_effects=True),
    )(points, slab)


def solution(mesh):
    placed = (P(("grp", "mem"), None), P("mem", None))
    return jax.shard_map(
        shards, mesh=mesh, in_specs=placed, out_specs=P(("grp", "mem"), None), check_vma=False
    )
```
